32 devices in a mesh: ctx: 16 (over z, x, core), head: 2 (over y).
Axes of the slice: x: 2, y: 2, z: 4, core: 2. Of those that a mesh axis runs over, the one named last changes fastest.
Arguments:
- q_absorbed: bfloat16 [2048, 64, 576], P('ctx', 'head'), may hold values from -6 to 6
- grad_out: bfloat16 [2048, 64, 512], P('ctx', 'head'), may hold values from -6 to 6
- log_norm: float32 [2048, 64], P('ctx', 'head'), may hold values from 5 to 7
- out_dot: float32 [2048, 64], P('ctx', 'head'), may hold values from -6 to 6
- kv_cache: bfloat16 [2048, 576], P(('ctx', 'head')), may hold values from -6 to 6
- block_links: int32 [16, 4], P('ctx'), may hold values 0 or 1
Outputs:
- d_query: bfloat16 [2048, 64, 576], P('ctx', 'head')
- d_kv: bfloat16 [2048, 576], P(('ctx', 'head'))
The draws below stay inside these ranges and needn't reach their ends.
All inputs are finite; a program needn't handle non-finite values. No bound on the sum of `block_links` on one device may be relied on, other than what follows from the above.
Results may differ from the reference program's by a relative error of at most 0.0061.
Values may be sent and summed in bfloat16 or wider, within the bound.
A program may use at most 128 MiB of HBM per device.

```python
import jax
import jax.numpy as jnp
from jax import lax

LAT = 512
ROPE = 64
HEADS = 64
OFFS = 4
TOK_DEV = 128
TOKENS = 2048
N_CTX = 16


def place_ends(array, own_key, low, high):
    index_at = [jax.random.randint(jax.random.fold_in(own_key, axis), (), 0, length) for axis, length in enumerate(array.shape)]
    main_axis = array.shape.index(max(array.shape))
    neighbour = index_at[:main_axis] + [(index_at[main_axis] + 1) % array.shape[main_axis]] + index_at[main_axis + 1:]
    return array.at[tuple(index_at)].set(low).at[tuple(neighbour)].set(high)


def block_levels(rng, extent, shards, low, top_value):
    gain, own = 1.0, jax.random.fold_in(rng, 6)
    for dim, shards_of in shards:
        heights = jnp.exp(jax.random.uniform(jax.random.fold_in(own, dim), (shards_of,), jnp.float32, low / len(shards), top_value / len(shards)))
        gain = gain * jnp.repeat(heights, extent[dim] // shards_of).reshape([-1 if axis == dim else 1 for axis in range(len(extent))])
    return gain


def normal_values(own_key, extent, scale, limit, shards=(), held_as=jnp.bfloat16):
    entries = scale * jax.random.normal(own_key, extent, jnp.float32)
    if shards:
        entries = entries * block_levels(own_key, extent, shards, -0.22, 0.18)
    return jnp.clip(entries, -limit, limit).astype(held_as)


def setup_inputs(seed: int = 0) -> dict:
    key_list = jax.random.split(jax.random.key(seed), 7)
    q_absorbed = normal_values(key_list[0], (TOKENS, HEADS, LAT + ROPE), 1.0, 6.0, ((0, 16), (1, 2)))
    grad_out = normal_values(key_list[1], (TOKENS, HEADS, LAT), 1.0, 6.0, ((0, 16), (1, 2)))
    log_norm = jnp.clip(5.0 + 2.0 * jax.random.uniform(key_list[2], (TOKENS, HEADS), jnp.float32) ** block_levels(key_list[2], (TOKENS, HEADS), ((0, 16), (1, 2)), -0.2, 0.2), 5.0, 7.0)
    out_dot = normal_values(key_list[3], (TOKENS, HEADS), 1.0, 6.0, ((0, 16), (1, 2)), jnp.float32)
    kv_cache = normal_values(key_list[4], (TOKENS, LAT + ROPE), 1.0, 6.0, ((0, 32),))
    block_links = place_ends((jax.random.randint(key_list[5], (N_CTX, OFFS), 0, 4) < 3).astype(jnp.int32), jax.random.fold_in(key_list[5], 1), 0, 1)
    return dict(q_absorbed=q_absorbed, grad_out=grad_out, log_norm=log_norm, out_dot=out_dot, kv_cache=kv_cache, block_links=block_links)


offset_list = (0, 1, 2, 8)


def block_terms(query_rows, grad_rows, norm_rows, dot_rows, key_rows, live_flag, causal):
    lat_width = grad_rows.shape[2]
    score_scale = query_rows.shape[2] ** -0.5
    query_f32 = query_rows.astype(jnp.float32)
    grad_f32 = grad_rows.astype(jnp.float32)
    key_f32 = key_rows.astype(jnp.float32)
    scores = jnp.einsum("thc,kc->thk", query_f32, key_f32) * score_scale
    keep_mask = jnp.broadcast_to(live_flag > 0, scores.shape)
    if causal:
        row_pos = lax.broadcasted_iota(jnp.int32, scores.shape, 0)
        col_pos = lax.broadcasted_iota(jnp.int32, scores.shape, 2)
        keep_mask = keep_mask & (row_pos >= col_pos)
    attn_prob = jnp.where(keep_mask, jnp.exp(scores - norm_rows[:, :, None]), 0.0)
    grad_prob = jnp.einsum("thl,kl->thk", grad_f32, key_f32[:, :lat_width])
    grad_score = (attn_prob * (grad_prob - dot_rows[:, :, None]) * score_scale).astype(jnp.bfloat16).astype(jnp.float32)
    prob_rounded = attn_prob.astype(jnp.bfloat16).astype(jnp.float32)
    query_term = jnp.einsum("thk,kc->thc", grad_score, key_f32)
    key_term = jnp.einsum("thk,thc->kc", grad_score, query_f32)
    value_term = jnp.einsum("thk,thl->kl", prob_rounded, grad_f32)
    key_term = key_term + jnp.pad(value_term, ((0, 0), (0, key_rows.shape[1] - lat_width)))
    return query_term, key_term


def reference(q_absorbed, grad_out, log_norm, out_dot, kv_cache, block_links):
    def one_block(block, carry):
        grads_q, grads_kv = carry
        start_row = (block * TOK_DEV).astype(jnp.int32)
        query_rows = lax.dynamic_slice_in_dim(q_absorbed, start_row, TOK_DEV, 0)
        grad_rows = lax.dynamic_slice_in_dim(grad_out, start_row, TOK_DEV, 0)
        norm_rows = lax.dynamic_slice_in_dim(log_norm, start_row, TOK_DEV, 0)
        dot_rows = lax.dynamic_slice_in_dim(out_dot, start_row, TOK_DEV, 0)
        summed = jnp.zeros(query_rows.shape, jnp.float32)
        for position, offset in enumerate(offset_list):
            source = (((block - offset) % N_CTX) * TOK_DEV).astype(jnp.int32)
            key_rows = lax.dynamic_slice_in_dim(kv_cache, source, TOK_DEV, 0)
            query_term, key_term = block_terms(query_rows, grad_rows, norm_rows, dot_rows, key_rows, block_links[block, position], offset == 0)
            summed = summed + query_term
            current = lax.dynamic_slice_in_dim(grads_kv, source, TOK_DEV, 0)
            grads_kv = lax.dynamic_update_slice_in_dim(grads_kv, current + key_term, source, 0)
        grads_q = lax.dynamic_update_slice_in_dim(grads_q, summed.astype(jnp.bfloat16), start_row, 0)
        return grads_q, grads_kv

    initial = (jnp.zeros(q_absorbed.shape, jnp.bfloat16), jnp.zeros(kv_cache.shape, jnp.float32))
    grads_q, grads_kv = lax.fori_loop(0, N_CTX, one_block, initial)
    return grads_q, grads_kv.astype(jnp.bfloat16)
```

```python
import functools
import math

import jax
import jax.numpy as jnp
from jax import lax
from jax.experimental import pallas as pl
from jax.experimental.pallas import tpu as pltpu
from jax.sharding import PartitionSpec as P

offset_list = (0, 1, 2, 8)
F32 = jnp.float32
BF16 = jnp.bfloat16


def dot(a, b, ca, cb):
    return lax.dot_general(a, b, (((ca,), (cb,)), ((), ())), preferred_element_type=F32)


MESH = pl.DeviceIdType.MESH
FIRST, LAST = (0, 2), (2, 4)
TILE = 16


def fused_kernel(
    n_ctx, n_head, links, kv_hbm, q_hbm, g_hbm, ln_hbm, od_hbm,
    dqv, dkv_ref,
    qv, graw, perm, gv, ln_ref, od_ref, dsv, pbv, acc, kvbuf, away, yrecv, fwd, crecv, drecv,
    q_sem, g_sem, in_sem, gs_s, gs_r, fw_s, fw_r, ry_s, ry_r, rc_s, rc_r, rd_s, rd_r,
):
    me = lax.axis_index("ctx")
    head = lax.axis_index("head")
    steps, group, feat, toks = qv.shape
    chunks, width, heads, lat = graw.shape
    cols = group * toks
    n_off, _, part, _ = kvbuf.shape
    blk = n_head * part
    scale = feat ** (-0.5)
    log2e = math.log2(math.e)

    def load_g(i):
        return pltpu.make_async_copy(g_hbm.at[pl.ds(i * width, width)], graw.at[i], g_sem.at[i])

    def load_q(i):
        return pltpu.make_async_copy(q_hbm.at[pl.ds(i * group, group)], qv.at[i], q_sem.at[i])

    def loop(start, stop, body):
        def run(i, carry):
            body(i)
            return carry

        lax.fori_loop(start, stop, run, 0)

    def peer(by, j=0):
        return (lax.rem(me + by + n_ctx, n_ctx), lax.rem(head + j + n_head, n_head))

    def send(src, dst, s_sem, r_sem, where):
        return pltpu.make_async_remote_copy(
            src_ref=src, dst_ref=dst, send_sem=s_sem, recv_sem=r_sem, device_id=where, device_id_type=MESH
        )

    for i in range(chunks):
        load_g(i).start()
    own = pltpu.make_async_copy(kv_hbm, kvbuf.at[0, 0], in_sem.at[0])
    norms = pltpu.make_async_copy(ln_hbm, ln_ref, in_sem.at[1])
    dots = pltpu.make_async_copy(od_hbm, od_ref, in_sem.at[2])

    places = {(by % n_ctx, 0) for o in offset_list[1:] for by in (o, -o)}
    places |= {(by % n_ctx, j) for by in (offset_list[1], -offset_list[1]) for j in range(1, n_head)}
    places |= {(0, j) for j in range(1, n_head)}
    barrier = pltpu.get_barrier_semaphore()
    for by, j in sorted(places):
        pl.semaphore_signal(barrier, inc=1, device_id=peer(by, j), device_id_type=MESH)
    for copy in (own, norms, dots):
        copy.start()
    for i in range(steps):
        load_q(i).start()

    rows = perm.shape[0]
    out_row = lax.broadcasted_iota(jnp.int32, (rows, rows), 0)
    in_row = lax.broadcasted_iota(jnp.int32, (rows, rows), 1)
    in_head = lax.rem(in_row, heads)
    perm[...] = jnp.where(out_row * heads == in_head * (rows - 1) + in_row, 1.0, 0.0).astype(BF16)
    acc[...] = jnp.zeros_like(acc)

    gather = [
        send(kv_hbm, kvbuf.at[pos, 0], gs_s.at[pos - 1], gs_r.at[pos - 1], peer(offset_list[pos]))
        for pos in range(1, n_off)
    ]
    spread = [
        [
            send(kv_hbm if pos == 0 else kvbuf.at[pos, 0], kvbuf.at[pos, j],
                 fw_s.at[pos, j - 1], fw_r.at[pos, j - 1], peer(0, -j))
            for j in range(1, n_head)
        ]
        for pos in range(n_off)
    ]
    pl.semaphore_wait(barrier, len(places))
    for copy in spread[0]:
        copy.start()
    for copy in [gather[0]] + gather[:0:-1]:
        copy.start()

    def relayout(i):
        load_g(i).wait()
        size = rows // heads
        tile = max(TILE, size)
        for start in range(0, width, tile):
            parts = []
            for s in range(start, start + tile, size):
                block = graw[i, s : s + size].reshape(rows, lat)
                parts.append(dot(perm[...], block, 1, 0).reshape(heads, size, lat))
            moved = jnp.concatenate(parts, 1).astype(BF16)
            for h in range(heads):
                gv[h // group, h % group, pl.ds(pl.multiple_of(i * width + start, tile), tile), :] = moved[h]

    def scores(i, low, high):
        keys = kvbuf[low:high].reshape((high - low) * blk, feat)
        q = jnp.concatenate([qv[i, k] for k in range(group)], 1)
        g = gv[i].reshape(cols, lat)
        ln = jnp.concatenate([ln_ref[i, k : k + 1, :] for k in range(group)], 1) * log2e
        od = jnp.concatenate([od_ref[i, k : k + 1, :] for k in range(group)], 1)
        s = dot(keys, q, 1, 0)
        dp = dot(keys[:, :lat], g, 1, 1)
        ps, dss = [], []
        for pos in range(low, high):
            sl = slice((pos - low) * blk, (pos - low + 1) * blk)
            bias = jnp.where(links[0, pos] > 0, ln, 1e30)
            p = jnp.exp2(s[sl] * (scale * log2e) - bias)
            if offset_list[pos] == 0:
                key = lax.broadcasted_iota(jnp.int32, p.shape, 0) + head * part
                key = jnp.where(key >= blk, key - blk, key)
                tok = lax.rem(lax.broadcasted_iota(jnp.int32, p.shape, 1), toks)
                p = jnp.where(tok >= key, p, 0.0)
            ps.append(p.astype(BF16))
            dss.append((p * (dp[sl] - od) * scale).astype(BF16))
        return jnp.concatenate(ps, 0), jnp.concatenate(dss, 0), q, g

    def key_terms(pb, ds, q, g, low, high):
        span = slice(low * blk, high * blk)
        dk = dot(ds, q, 1, 1)
        dv = dot(pb, g, 1, 0)
        acc[span, :lat] += dk[:, :lat] + dv
        acc[span, lat:] += dk[:, lat:]

    def rows_of(pos, j):
        return acc[pos * blk + j * part : pos * blk + (j + 1) * part, :]

    across = [
        [
            send(away.at[j - 1, pos], yrecv.at[j - 1, pos], ry_s.at[pos, j - 1], ry_r.at[pos, j - 1], peer(0, j))
            for j in range(1, n_head)
        ]
        for pos in range(n_off)
    ]
    back = [
        send(fwd.at[pos - 1], crecv.at[pos - 1], rc_s.at[pos - 1], rc_r.at[pos - 1], peer(-offset_list[pos]))
        for pos in range(1, n_off)
    ]
    skew = [
        send(away.at[j - 1, 1], drecv.at[j - 1], rd_s.at[j - 1], rd_r.at[j - 1], peer(-offset_list[1], j))
        for j in range(1, n_head)
    ]

    def start(copies):
        for copy in copies:
            copy.start()

    def arrive(copies):
        for copy in copies:
            copy.wait_recv()

    def pack(pos):
        for j in range(1, n_head):
            away[j - 1, pos] = rows_of(pos, j).astype(BF16)

    def folded(pos):
        arrive(across[pos])
        total = rows_of(pos, 0)
        for j in range(1, n_head):
            total = total + yrecv[j - 1, pos].astype(F32)
        return total

    def first(i):
        pb, ds, _, _ = scores(i, *FIRST)
        dsv[i, : FIRST[1] * blk, :] = ds
        pbv[i] = pb

    def second(i):
        pb, ds, q, g = scores(i, *LAST)
        dsv[i, LAST[0] * blk : LAST[1] * blk, :] = ds
        key_terms(pb, ds, q, g, *LAST)

    def third(i):
        q = jnp.concatenate([qv[i, k] for k in range(group)], 1)
        key_terms(pbv[i], dsv[i, : FIRST[1] * blk, :], q, gv[i].reshape(cols, lat), *FIRST)

    def fourth(i):
        keys = kvbuf[...].reshape(n_off * blk, feat)
        dq = dot(keys, dsv[i], 0, 0).astype(BF16)
        for k in range(group):
            dqv[i, k] = dq[:, k * toks : (k + 1) * toks]

    loop(0, chunks, relayout)
    for copy in (own, norms, dots):
        copy.wait()
    for i in range(steps):
        load_q(i).wait()
    arrive([gather[0]])
    start(spread[1])
    arrive(spread[0] + spread[1])
    loop(0, steps // 2, first)
    for pos in range(*LAST)[::-1]:
        arrive([gather[pos - 1]])
        start(spread[pos])
    loop(steps // 2, steps, first)
    arrive(spread[2] + spread[3])
    loop(0, steps, second)
    for pos in range(*LAST)[::-1]:
        pack(pos)
        start(across[pos])
    loop(0, steps // 2, third)
    fwd[2] = folded(3).astype(BF16)
    start([back[2]])
    loop(steps // 2, steps, third)
    pack(1)
    fwd[0] = rows_of(1, 0).astype(BF16)
    start(skew + [back[0]])
    pack(0)
    start(across[0])
    fwd[1] = folded(2).astype(BF16)
    start([back[1]])
    loop(0, steps, fourth)
    total = folded(0)
    for copy in gather + sum(spread, []) + sum([across[p] for p in (0, 2, 3)], []):
        copy.wait_send()
    for copy in skew + back:
        copy.wait()
    for j in range(1, n_head):
        total = total + drecv[j - 1].astype(F32)
    for pos in range(1, n_off):
        total = total + crecv[pos - 1].astype(F32)
    dkv_ref[...] = total.astype(BF16)


def graw_rows(heads):
    return max(8, 256 // heads) * heads


def fused(n_ctx, n_head, q, g, ln, od, kv, links, group=8, width=32):
    heads, feat, toks = q.shape
    lat = g.shape[2]
    part = kv.shape[0]
    n_off = len(offset_list)
    group = math.gcd(group, heads)
    width = math.gcd(width, toks)
    steps, chunks = heads // group, toks // width
    cols, keys = group * toks, n_off * n_head * part
    near = FIRST[1] * n_head * part
    rows = graw_rows(heads)
    dma = pltpu.SemaphoreType.DMA
    hbm = pl.BlockSpec(memory_space=pl.ANY)
    vmem = pl.BlockSpec(memory_space=pltpu.VMEM)
    return pl.pallas_call(
        functools.partial(fused_kernel, n_ctx, n_head),
        in_specs=[pl.BlockSpec(memory_space=pltpu.SMEM), hbm, hbm, hbm, hbm, hbm],
        out_specs=[vmem, vmem],
        out_shape=[
            pltpu.VMEM((steps, group, feat, toks), BF16),
            jax.ShapeDtypeStruct((part, feat), BF16),
        ],
        scratch_shapes=[
            pltpu.VMEM((steps, group, feat, toks), BF16),
            pltpu.VMEM((chunks, width, heads, lat), BF16),
            pltpu.VMEM((rows, rows), BF16),
            pltpu.VMEM((steps, group, toks, lat), BF16),
            pltpu.VMEM((steps, group, toks), F32),
            pltpu.VMEM((steps, group, toks), F32),
            pltpu.VMEM((steps, keys, cols), BF16),
            pltpu.VMEM((steps, near, cols), BF16),
            pltpu.VMEM((keys, feat), F32),
            pltpu.VMEM((n_off, n_head, part, feat), BF16),
            pltpu.VMEM((n_head - 1, n_off, part, feat), BF16),
            pltpu.VMEM((n_head - 1, n_off, part, feat), BF16),
            pltpu.VMEM((n_off - 1, part, feat), BF16),
            pltpu.VMEM((n_off - 1, part, feat), BF16),
            pltpu.VMEM((n_head - 1, part, feat), BF16),
            dma((steps,)),
            dma((chunks,)),
            dma((3,)),
            dma((n_off - 1,)),
            dma((n_off - 1,)),
            dma((n_off, n_head - 1)),
            dma((n_off, n_head - 1)),
            dma((n_off, n_head - 1)),
            dma((n_off, n_head - 1)),
            dma((n_off - 1,)),
            dma((n_off - 1,)),
            dma((n_head - 1,)),
            dma((n_head - 1,)),
        ],
        compiler_params=pltpu.CompilerParams(
            collective_id=0, has_side_effects=True, vmem_limit_bytes=67043328 - 2 * heads * feat * toks - 16384
        ),
        cost_estimate=pl.CostEstimate(flops=12 * 10**9, bytes_accessed=14 * 10**6, transcendentals=2 * 10**6),
        name="mla_bwd",
    )(links, kv, q, g, ln.reshape(steps, group, toks), od.reshape(steps, group, toks))


def shards(q, g, ln, od, kv, links):
    dq, dkv = fused(
        lax.axis_size("ctx"),
        lax.axis_size("head"),
        jnp.transpose(q, (1, 2, 0)),
        g,
        ln.T,
        od.T,
        kv,
        links,
    )
    return jnp.transpose(dq.reshape(-1, *dq.shape[2:]), (2, 0, 1)), dkv


def solution(mesh):
    in_specs = (
        P("ctx", "head", None),
        P("ctx", "head", None),
        P("ctx", "head"),
        P("ctx", "head"),
        P(("ctx", "head"), None),
        P("ctx", None),
    )
    out_specs = (P("ctx", "head", None), P(("ctx", "head"), None))
    return jax.shard_map(shards, mesh=mesh, in_specs=in_specs, out_specs=out_specs, check_vma=False)
```

```python
import functools
import math

import jax
import jax.numpy as jnp
from jax import lax
from jax.experimental import pallas as pl
from jax.experimental.pallas import tpu as pltpu
from jax.sharding import PartitionSpec as P

F32 = jnp.float32
BF16 = jnp.bfloat16


def dot(a, b, ca, cb):
    return lax.dot_general(a, b, (((ca,), (cb,)), ((), ())), preferred_element_type=F32)


MESH = pl.DeviceIdType.MESH
TILE = 16
GROUP = 8
SLOTS = ((0, 0), (1, 1), (2, 2), (8, 3))
GO = (2, 3)
PLAN = (
    ("have", 0), ("sckt", 0, 1, 0, 2), ("relay", 2), ("hop", 0), ("relay", 3), ("sckt", 0, 1, 2, 3),
    ("have", 2), ("hop", 1), ("sckt", 0, 1, 3, 4), ("have", 3), ("sckt", 2, 4, 0, 4), ("fold", 3), ("fold", 2),
    ("fold", 0), ("have", 1), ("sckt", 1, 2, 0, 2), ("pass", 3), ("sckt", 1, 2, 2, 3), ("pass", 2),
    ("sckt", 1, 2, 3, 4), ("direct", 1), ("dq", 0, 4),
)


def fused_kernel(
    n_ctx, n_head, links, kv_hbm, q_hbm, g_hbm, ln_hbm, od_hbm,
    dqv, dkv_ref,
    qv, graw, perm, gv, ln_ref, od_ref, dsv, pbv, acc, kvbuf, away, yrecv, fwd, crecv, drecv,
    q_sem, g_sem, in_sem, gs_s, gs_r, fw_s, fw_r, ry_s, ry_r, rc_s, rc_r, rd_s, rd_r,
):
    me = lax.axis_index("ctx")
    head = lax.axis_index("head")
    steps, group, feat, toks = qv.shape
    chunks, width, heads, lat = graw.shape
    cols = group * toks
    n_off, _, part, _ = kvbuf.shape
    blk = n_head * part
    scale = feat ** (-0.5)
    log2e = math.log2(math.e)

    def load_g(i):
        return pltpu.make_async_copy(g_hbm.at[pl.ds(i * width, width)], graw.at[i], g_sem.at[i])

    def load_q(i):
        return pltpu.make_async_copy(q_hbm.at[pl.ds(i * group, group)], qv.at[i], q_sem.at[i])

    def loop(start, stop, body):
        def run(i, carry):
            body(i)
            return carry

        if stop > start:
            lax.fori_loop(start, stop, run, 0)

    def peer(by, j=0):
        return (lax.rem(me + by + n_ctx, n_ctx), lax.rem(head + j + n_head, n_head))

    def send(src, dst, s_sem, r_sem, where):
        return pltpu.make_async_remote_copy(
            src_ref=src, dst_ref=dst, send_sem=s_sem, recv_sem=r_sem, device_id=where, device_id_type=MESH
        )

    for i in range(chunks):
        load_g(i).start()
    own = pltpu.make_async_copy(kv_hbm, kvbuf.at[0, 0], in_sem.at[0])
    norms = pltpu.make_async_copy(ln_hbm, ln_ref, in_sem.at[1])
    dots = pltpu.make_async_copy(od_hbm, od_ref, in_sem.at[2])

    odd = lax.rem(me, 2)
    places = [(-o, 0) for o, _ in SLOTS[2:]] + [(0, j) for j in range(1, n_head)] + [(1 - 2 * odd, 0)]
    barrier = pltpu.get_barrier_semaphore()
    for by, j in places:
        pl.semaphore_signal(barrier, inc=1, device_id=peer(by, j), device_id_type=MESH)
    for copy in (own, norms, dots):
        copy.start()
    for i in range(steps):
        load_q(i).start()

    rows = perm.shape[0]
    out_row = lax.broadcasted_iota(jnp.int32, (rows, rows), 0)
    in_row = lax.broadcasted_iota(jnp.int32, (rows, rows), 1)
    in_head = lax.rem(in_row, heads)
    perm[...] = jnp.where(out_row * heads == in_head * (rows - 1) + in_row, 1.0, 0.0).astype(BF16)
    acc[...] = jnp.zeros_like(acc)

    gather = [
        send(kv_hbm, kvbuf.at[pos, 0], gs_s.at[pos - 1], gs_r.at[pos - 1], peer(SLOTS[pos][0]))
        for pos in range(1, n_off)
    ]
    spread = [
        [
            send(kv_hbm if pos == 0 else kvbuf.at[pos, 0], kvbuf.at[pos, j],
                 fw_s.at[pos, j - 1], fw_r.at[pos, j - 1], peer(0, -j))
            for j in range(1, n_head)
        ]
        for pos in range(n_off)
    ]
    pl.semaphore_wait(barrier, len(places))
    for copy in [gather[p - 1] for p in GO] + spread[0]:
        copy.start()
    hops = [
        send(kvbuf.at[2 * odd, j], kvbuf.at[1, j], gs_s.at[0] if j == 0 else fw_s.at[1, j - 1],
             gs_r.at[0] if j == 0 else fw_r.at[1, j - 1], peer(1 - 2 * odd))
        for j in range(n_head)
    ]

    def relayout(i):
        load_g(i).wait()
        size = rows // heads
        tile = max(TILE, size)
        for start in range(0, width, tile):
            parts = []
            for s in range(start, start + tile, size):
                block = graw[i, s : s + size].reshape(rows, lat)
                parts.append(dot(perm[...], block, 1, 0).reshape(heads, size, lat))
            moved = jnp.concatenate(parts, 1).astype(BF16)
            for h in range(heads):
                gv[h // group, h % group, pl.ds(pl.multiple_of(i * width + start, tile), tile), :] = moved[h]

    def scores(i, low, high):
        keys = kvbuf[low:high].reshape((high - low) * blk, feat)
        q = jnp.concatenate([qv[i, k] for k in range(group)], 1)
        g = gv[i].reshape(cols, lat)
        ln = jnp.concatenate([ln_ref[i, k : k + 1, :] for k in range(group)], 1) * log2e
        od = jnp.concatenate([od_ref[i, k : k + 1, :] for k in range(group)], 1)
        s = dot(keys, q, 1, 0)
        dp = dot(keys[:, :lat], g, 1, 1)
        ps, dss = [], []
        for pos in range(low, high):
            sl = slice((pos - low) * blk, (pos - low + 1) * blk)
            bias = jnp.where(links[0, SLOTS[pos][1]] > 0, ln, 1e30)
            p = jnp.exp2(s[sl] * (scale * log2e) - bias)
            if SLOTS[pos][0] == 0:
                key = lax.broadcasted_iota(jnp.int32, p.shape, 0) + head * part
                key = jnp.where(key >= blk, key - blk, key)
                tok = lax.rem(lax.broadcasted_iota(jnp.int32, p.shape, 1), toks)
                p = jnp.where(tok >= key, p, 0.0)
            ps.append(p.astype(BF16))
            dss.append((p * (dp[sl] - od) * scale).astype(BF16))
        return jnp.concatenate(ps, 0), jnp.concatenate(dss, 0), q, g

    def key_terms(pb, ds, q, g, low, high):
        span = slice(low * blk, high * blk)
        dk = dot(ds, q, 1, 1)
        dv = dot(pb, g, 1, 0)
        acc[span, :lat] += dk[:, :lat] + dv
        acc[span, lat:] += dk[:, lat:]

    def rows_of(pos, j):
        return acc[pos * blk + j * part : pos * blk + (j + 1) * part, :]

    across = [
        [
            send(away.at[j - 1, pos], yrecv.at[j - 1, pos], ry_s.at[pos, j - 1], ry_r.at[pos, j - 1], peer(0, j))
            for j in range(1, n_head)
        ]
        for pos in range(n_off)
    ]
    back = [
        send(fwd.at[pos - 1], crecv.at[pos - 1], rc_s.at[pos - 1], rc_r.at[pos - 1], peer(-SLOTS[pos][0]))
        for pos in range(1, n_off)
    ]
    skew = [
        [
            send(away.at[j - 1, pos], drecv.at[pos - 1, j - 1], rd_s.at[pos - 1, j - 1], rd_r.at[pos - 1, j - 1],
                 peer(-SLOTS[pos][0], j))
            for j in range(1, n_head)
        ]
        for pos in range(1, n_off)
    ]

    def start(copies):
        for copy in copies:
            copy.start()

    def arrive(copies):
        for copy in copies:
            copy.wait_recv()

    def relay(pos):
        arrive([gather[pos - 1]])
        start(spread[pos])

    def have(pos):
        arrive(hops if pos == 1 else spread[pos])

    def hop(part):
        if part == 0:
            start(hops[:1])
        else:
            start(hops[1:])

    def issue(pos):
        start([gather[pos - 1]])

    def fold(pos):
        for j in range(1, n_head):
            away[j - 1, pos] = rows_of(pos, j).astype(BF16)
        start(across[pos])

    def folded(pos):
        arrive(across[pos])
        total = rows_of(pos, 0)
        for j in range(1, n_head):
            total = total + yrecv[j - 1, pos].astype(F32)
        return total

    def onward(pos):
        fwd[pos - 1] = folded(pos).astype(BF16)
        start([back[pos - 1]])

    def direct(pos):
        for j in range(1, n_head):
            away[j - 1, pos] = rows_of(pos, j).astype(BF16)
        fwd[pos - 1] = rows_of(pos, 0).astype(BF16)
        start(skew[pos - 1] + [back[pos - 1]])

    def query(i):
        return jnp.concatenate([qv[i, k] for k in range(group)], 1)

    def sc(i, low, high):
        pb, ds, _, _ = scores(i, low, high)
        dsv[i, low * blk : high * blk, :] = ds
        pbv[i, low * blk : high * blk, :] = pb

    def sckt(i, low, high):
        pb, ds, q, g = scores(i, low, high)
        dsv[i, low * blk : high * blk, :] = ds
        key_terms(pb, ds, q, g, low, high)

    def kt(i, low, high):
        span = slice(low * blk, high * blk)
        key_terms(pbv[i, span, :], dsv[i, span, :], query(i), gv[i].reshape(cols, lat), low, high)

    def dq(i):
        keys = kvbuf[...].reshape(n_off * blk, feat)
        out = dot(keys, dsv[i], 0, 0).astype(BF16)
        for k in range(group):
            dqv[i, k] = out[:, k * toks : (k + 1) * toks]

    def scaled(part):
        return part * steps // 4

    loop(0, chunks, relayout)
    for copy in (own, norms, dots):
        copy.wait()
    for i in range(steps):
        load_q(i).wait()
    calls = {"relay": relay, "have": have, "fold": fold, "pass": onward, "direct": direct, "hop": hop, "issue": issue}
    loops = {"sc": sc, "kt": kt, "sckt": sckt}
    sent, got = gather[1:] + spread[0] + sum(spread[2:], []) + hops, []
    for name, *args in PLAN:
        if name == "dq":
            loop(scaled(args[0]), scaled(args[1]), dq)
        elif name in loops:
            low, high, first, last = args
            loop(scaled(first), scaled(last), lambda i, name=name, low=low, high=high: loops[name](i, low, high))
        else:
            calls[name](*args)
            pos = args[0]
            if name == "fold":
                sent += across[pos]
            elif name == "pass":
                sent, got = sent + [back[pos - 1]], got + [back[pos - 1]]
            elif name == "direct":
                both = skew[pos - 1] + [back[pos - 1]]
                sent, got = sent + both, got + both
    total = folded(0)
    for copy in sent:
        copy.wait_send()
    arrive(got)
    directs = [args[0] for name, *args in PLAN if name == "direct"]
    for pos in directs:
        for j in range(1, n_head):
            total = total + drecv[pos - 1, j - 1].astype(F32)
    for pos in range(1, n_off):
        total = total + crecv[pos - 1].astype(F32)
    dkv_ref[...] = total.astype(BF16)


def graw_rows(heads):
    return max(8, 256 // heads) * heads


def fused(n_ctx, n_head, q, g, ln, od, kv, links, group=GROUP, width=32):
    heads, feat, toks = q.shape
    lat = g.shape[2]
    part = kv.shape[0]
    n_off = len(SLOTS)
    group = math.gcd(group, heads)
    width = math.gcd(width, toks)
    steps, chunks = heads // group, toks // width
    cols, keys = group * toks, n_off * n_head * part
    rows = graw_rows(heads)
    dma = pltpu.SemaphoreType.DMA
    hbm = pl.BlockSpec(memory_space=pl.ANY)
    vmem = pl.BlockSpec(memory_space=pltpu.VMEM)
    return pl.pallas_call(
        functools.partial(fused_kernel, n_ctx, n_head),
        in_specs=[pl.BlockSpec(memory_space=pltpu.SMEM), hbm, hbm, hbm, hbm, hbm],
        out_specs=[vmem, vmem],
        out_shape=[
            pltpu.VMEM((steps, group, feat, toks), BF16),
            jax.ShapeDtypeStruct((part, feat), BF16),
        ],
        scratch_shapes=[
            pltpu.VMEM((steps, group, feat, toks), BF16),
            pltpu.VMEM((chunks, width, heads, lat), BF16),
            pltpu.VMEM((rows, rows), BF16),
            pltpu.VMEM((steps, group, toks, lat), BF16),
            pltpu.VMEM((steps, group, toks), F32),
            pltpu.VMEM((steps, group, toks), F32),
            pltpu.VMEM((steps, keys, cols), BF16),
            pltpu.VMEM((steps, keys, cols), BF16),
            pltpu.VMEM((keys, feat), F32),
            pltpu.VMEM((n_off, n_head, part, feat), BF16),
            pltpu.VMEM((n_head - 1, n_off, part, feat), BF16),
            pltpu.VMEM((n_head - 1, n_off, part, feat), BF16),
            pltpu.VMEM((n_off - 1, part, feat), BF16),
            pltpu.VMEM((n_off - 1, part, feat), BF16),
            pltpu.VMEM((n_off - 1, n_head - 1, part, feat), BF16),
            dma((steps,)),
            dma((chunks,)),
            dma((3,)),
            dma((n_off - 1,)),
            dma((n_off - 1,)),
            dma((n_off, n_head - 1)),
            dma((n_off, n_head - 1)),
            dma((n_off, n_head - 1)),
            dma((n_off, n_head - 1)),
            dma((n_off - 1,)),
            dma((n_off - 1,)),
            dma((n_off - 1, n_head - 1)),
            dma((n_off - 1, n_head - 1)),
        ],
        compiler_params=pltpu.CompilerParams(
            collective_id=0, has_side_effects=True, vmem_limit_bytes=67043328 - 2 * heads * feat * toks - 16384
        ),
        cost_estimate=pl.CostEstimate(flops=12 * 10**9, bytes_accessed=14 * 10**6, transcendentals=2 * 10**6),
        name="mla_bwd",
    )(links, kv, q, g, ln.reshape(steps, group, toks), od.reshape(steps, group, toks))


def shards(q, g, ln, od, kv, links):
    dq, dkv = fused(
        lax.axis_size("ctx"),
        lax.axis_size("head"),
        jnp.transpose(q, (1, 2, 0)),
        g,
        ln.T,
        od.T,
        kv,
        links,
    )
    return jnp.transpose(dq.reshape(-1, *dq.shape[2:]), (2, 0, 1)), dkv


def solution(mesh):
    in_specs = (
        P("ctx", "head", None),
        P("ctx", "head", None),
        P("ctx", "head"),
        P("ctx", "head"),
        P(("ctx", "head"), None),
        P("ctx", None),
    )
    out_specs = (P("ctx", "head", None), P(("ctx", "head"), None))
    return jax.shard_map(shards, mesh=mesh, in_specs=in_specs, out_specs=out_specs, check_vma=False)
```

```python
import functools
import math

import jax
import jax.numpy as jnp
from jax import lax
from jax.experimental import pallas as pl
from jax.experimental.pallas import tpu as pltpu
from jax.sharding import PartitionSpec as P

F32 = jnp.float32
BF16 = jnp.bfloat16


def dot(a, b, ca, cb):
    return lax.dot_general(a, b, (((ca,), (cb,)), ((), ())), preferred_element_type=F32)


MESH = pl.DeviceIdType.MESH
TILE = 16
GROUP = 8
FLUSH = 1
PAIRED = ((2, 4), 'dq', (0, 1), (1, 2))
SLOTS = ((0, 0), (1, 1), (2, 2), (8, 3))
GO = (2, 3)
PLAN = (
    ("have", 0), ("sckt", 0, 1, 0, 2), ("relay", 2), ("hop", 0), ("relay", 3), ("sckt", 0, 1, 2, 3),
    ("have", 2), ("hop", 1), ("sckt", 0, 1, 3, 4), ("have", 3), ("sckt", 2, 4, 0, 4), ("fold", 3),
    ("fold", 2), ("have", 1), ("sckt", 1, 2, 0, 2), ("pass", 3), ("sckt", 1, 2, 2, 3), ("pass", 2),
    ("sckt", 1, 2, 3, 4), ("direct", 1), ("fold", 0), ("dq", 0, 4),
)


def fused_kernel(
    n_ctx, n_head, links, kv_hbm, q_hbm, g_hbm, ln_hbm, od_hbm,
    dqv, dkv_ref,
    qv, graw, perm, gv, ln_ref, od_ref, dsv, pbv, acc, kvbuf, away, yrecv, fwd, crecv, drecv,
    q_sem, g_sem, in_sem, gs_s, gs_r, fw_s, fw_r, ry_s, ry_r, rc_s, rc_r, rd_s, rd_r,
):
    me = lax.axis_index("ctx")
    head = lax.axis_index("head")
    steps, group, feat, toks = qv.shape
    chunks, width, heads, lat = graw.shape
    cols = group * toks
    n_off, _, part, _ = kvbuf.shape
    blk = n_head * part
    scale = feat ** (-0.5)
    log2e = math.log2(math.e)

    def load_g(i):
        return pltpu.make_async_copy(g_hbm.at[pl.ds(i * width, width)], graw.at[i], g_sem.at[i])

    def load_q(i):
        return pltpu.make_async_copy(q_hbm.at[pl.ds(i * group, group)], qv.at[i], q_sem.at[i])

    def loop(start, stop, body):
        def run(i, carry):
            body(i)
            return carry

        if stop > start:
            lax.fori_loop(start, stop, run, 0)

    def pairs(start, stop, body):
        whole = start + (stop - start) // 2 * 2

        def run(i, carry):
            body(start + 2 * i)
            body(start + 2 * i + 1)
            return carry

        if whole > start:
            lax.fori_loop(0, (whole - start) // 2, run, 0)
        loop(whole, stop, body)

    def peer(by, j=0):
        return (lax.rem(me + by + n_ctx, n_ctx), lax.rem(head + j + n_head, n_head))

    def send(src, dst, s_sem, r_sem, where):
        return pltpu.make_async_remote_copy(
            src_ref=src, dst_ref=dst, send_sem=s_sem, recv_sem=r_sem, device_id=where, device_id_type=MESH
        )

    for i in range(chunks):
        load_g(i).start()
    own = pltpu.make_async_copy(kv_hbm, kvbuf.at[0, 0], in_sem.at[0])
    norms = pltpu.make_async_copy(ln_hbm, ln_ref, in_sem.at[1])
    dots = pltpu.make_async_copy(od_hbm, od_ref, in_sem.at[2])

    odd = lax.rem(me, 2)
    places = [(-o, 0) for o, _ in SLOTS[2:]] + [(0, j) for j in range(1, n_head)] + [(1 - 2 * odd, 0)]
    barrier = pltpu.get_barrier_semaphore()
    for by, j in places:
        pl.semaphore_signal(barrier, inc=1, device_id=peer(by, j), device_id_type=MESH)
    for copy in (own, norms, dots):
        copy.start()
    for i in range(steps):
        load_q(i).start()

    rows = perm.shape[0]
    out_row = lax.broadcasted_iota(jnp.int32, (rows, rows), 0)
    in_row = lax.broadcasted_iota(jnp.int32, (rows, rows), 1)
    in_head = lax.rem(in_row, heads)
    perm[...] = jnp.where(out_row * heads == in_head * (rows - 1) + in_row, 1.0, 0.0).astype(BF16)
    acc[...] = jnp.zeros_like(acc)

    gather = [
        send(kv_hbm, kvbuf.at[pos, 0], gs_s.at[pos - 1], gs_r.at[pos - 1], peer(SLOTS[pos][0]))
        for pos in range(1, n_off)
    ]
    spread = [
        [
            send(kv_hbm if pos == 0 else kvbuf.at[pos, 0], kvbuf.at[pos, j],
                 fw_s.at[pos, j - 1], fw_r.at[pos, j - 1], peer(0, -j))
            for j in range(1, n_head)
        ]
        for pos in range(n_off)
    ]
    pl.semaphore_wait(barrier, len(places))
    for copy in [gather[p - 1] for p in GO] + spread[0]:
        copy.start()
    hops = [
        send(kvbuf.at[2 * odd, j], kvbuf.at[1, j], gs_s.at[0] if j == 0 else fw_s.at[1, j - 1],
             gs_r.at[0] if j == 0 else fw_r.at[1, j - 1], peer(1 - 2 * odd))
        for j in range(n_head)
    ]

    def relayout(i):
        load_g(i).wait()
        size = rows // heads
        tile = max(TILE, size)
        for start in range(0, width, tile):
            parts = []
            for s in range(start, start + tile, size):
                block = graw[i, s : s + size].reshape(rows, lat)
                parts.append(dot(perm[...], block, 1, 0).reshape(heads, size, lat))
            moved = jnp.concatenate(parts, 1).astype(BF16)
            for h in range(heads):
                gv[h // group, h % group, pl.ds(pl.multiple_of(i * width + start, tile), tile), :] = moved[h]

    def scores(i, low, high):
        keys = kvbuf[low:high].reshape((high - low) * blk, feat)
        q = jnp.concatenate([qv[i, k] for k in range(group)], 1)
        g = gv[i].reshape(cols, lat)
        ln = jnp.concatenate([ln_ref[i, k : k + 1, :] for k in range(group)], 1) * log2e
        od = jnp.concatenate([od_ref[i, k : k + 1, :] for k in range(group)], 1)
        s = dot(keys, q, 1, 0)
        dp = dot(keys[:, :lat], g, 1, 1)
        ps, dss = [], []
        for pos in range(low, high):
            sl = slice((pos - low) * blk, (pos - low + 1) * blk)
            bias = jnp.where(links[0, SLOTS[pos][1]] > 0, ln, 1e30)
            p = jnp.exp2(s[sl] * (scale * log2e) - bias)
            if SLOTS[pos][0] == 0:
                key = lax.broadcasted_iota(jnp.int32, p.shape, 0) + head * part
                key = jnp.where(key >= blk, key - blk, key)
                tok = lax.rem(lax.broadcasted_iota(jnp.int32, p.shape, 1), toks)
                p = jnp.where(tok >= key, p, 0.0)
            ps.append(p.astype(BF16))
            dss.append((p * (dp[sl] - od) * scale).astype(BF16))
        return jnp.concatenate(ps, 0), jnp.concatenate(dss, 0), q, g

    def key_terms(pb, ds, q, g, low, high):
        span = slice(low * blk, high * blk)
        dk = dot(ds, q, 1, 1)
        dv = dot(pb, g, 1, 0)
        acc[span, :lat] += dk[:, :lat] + dv
        acc[span, lat:] += dk[:, lat:]

    def rows_of(pos, j):
        return acc[pos * blk + j * part : pos * blk + (j + 1) * part, :]

    across = [
        [
            send(away.at[j - 1, pos], yrecv.at[j - 1, pos], ry_s.at[pos, j - 1], ry_r.at[pos, j - 1], peer(0, j))
            for j in range(1, n_head)
        ]
        for pos in range(n_off)
    ]
    back = [
        send(fwd.at[pos - 1], crecv.at[pos - 1], rc_s.at[pos - 1], rc_r.at[pos - 1], peer(-SLOTS[pos][0]))
        for pos in range(1, n_off)
    ]
    skew = [
        [
            send(away.at[j - 1, pos], drecv.at[pos - 1, j - 1], rd_s.at[pos - 1, j - 1], rd_r.at[pos - 1, j - 1],
                 peer(-SLOTS[pos][0], j))
            for j in range(1, n_head)
        ]
        for pos in range(1, n_off)
    ]

    def start(copies):
        for copy in copies:
            copy.start()

    def arrive(copies):
        for copy in copies:
            copy.wait_recv()

    def relay(pos):
        arrive([gather[pos - 1]])
        start(spread[pos])

    def have(pos):
        arrive(hops if pos == 1 else spread[pos])

    def hop(part):
        if part == 0:
            start(hops[:1])
        else:
            start(hops[1:])

    def issue(pos):
        start([gather[pos - 1]])

    def fold(pos):
        for j in range(1, n_head):
            away[j - 1, pos] = rows_of(pos, j).astype(BF16)
        start(across[pos])

    def folded(pos):
        arrive(across[pos])
        total = rows_of(pos, 0)
        for j in range(1, n_head):
            total = total + yrecv[j - 1, pos].astype(F32)
        return total

    def onward(pos):
        fwd[pos - 1] = folded(pos).astype(BF16)
        start([back[pos - 1]])

    def direct(pos):
        for j in range(1, n_head):
            away[j - 1, pos] = rows_of(pos, j).astype(BF16)
        fwd[pos - 1] = rows_of(pos, 0).astype(BF16)
        start(skew[pos - 1] + [back[pos - 1]])

    def query(i):
        return jnp.concatenate([qv[i, k] for k in range(group)], 1)

    def sc(i, low, high):
        pb, ds, _, _ = scores(i, low, high)
        dsv[i, low * blk : high * blk, :] = ds
        pbv[i, low * blk : high * blk, :] = pb

    def sckt(i, low, high):
        pb, ds, q, g = scores(i, low, high)
        dsv[i, low * blk : high * blk, :] = ds
        key_terms(pb, ds, q, g, low, high)

    def kt(i, low, high):
        span = slice(low * blk, high * blk)
        key_terms(pbv[i, span, :], dsv[i, span, :], query(i), gv[i].reshape(cols, lat), low, high)

    def dq(i):
        keys = kvbuf[...].reshape(n_off * blk, feat)
        out = dot(keys, dsv[i], 0, 0).astype(BF16)
        for k in range(group):
            dqv[i, k] = out[:, k * toks : (k + 1) * toks]

    def scaled(part):
        return part * steps // 4

    loop(0, chunks, relayout)
    for copy in (own, norms, dots):
        copy.wait()
    for i in range(steps):
        load_q(i).wait()
    calls = {"relay": relay, "have": have, "fold": fold, "pass": onward, "direct": direct, "hop": hop, "issue": issue}
    loops = {"sc": sc, "kt": kt, "sckt": sckt}
    sent, got = gather[1:] + spread[0] + sum(spread[2:], []) + hops, []
    for name, *args in PLAN:
        if name == "dq":
            (pairs if 'dq' in PAIRED else loop)(scaled(args[0]), scaled(args[1]), dq)
        elif name in loops:
            low, high, first, last = args
            (pairs if (low, high) in PAIRED else loop)(scaled(first), scaled(last), lambda i, name=name, low=low, high=high: loops[name](i, low, high))
        else:
            calls[name](*args)
            pos = args[0]
            if name == "fold":
                sent += across[pos]
            elif name == "pass":
                sent, got = sent + [back[pos - 1]], got + [back[pos - 1]]
            elif name == "direct":
                both = skew[pos - 1] + [back[pos - 1]]
                sent, got = sent + both, got + both
    total = folded(0)
    for copy in sent:
        copy.wait_send()
    arrive(got)
    directs = [args[0] for name, *args in PLAN if name == "direct"]
    for pos in directs:
        for j in range(1, n_head):
            total = total + drecv[pos - 1, j - 1].astype(F32)
    for pos in range(1, n_off):
        total = total + crecv[pos - 1].astype(F32)
    dkv_ref[...] = total.astype(BF16)


def graw_rows(heads):
    return max(8, 256 // heads) * heads


def flush_kernel(dq_ref, dkv_ref, dq_hbm, dkv_hbm, sem):
    steps, group = dq_ref.shape[:2]
    size = group // FLUSH
    copies = [pltpu.make_async_copy(dkv_ref, dkv_hbm, sem.at[steps * FLUSH])]
    for i in range(steps * FLUSH):
        cut = (i // FLUSH, pl.ds(i % FLUSH * size, size))
        copies.append(pltpu.make_async_copy(dq_ref.at[cut], dq_hbm.at[cut], sem.at[i]))
    for copy in copies:
        copy.start()
    for copy in copies:
        copy.wait()


def fused(n_ctx, n_head, q, g, ln, od, kv, links, group=GROUP, width=32):
    heads, feat, toks = q.shape
    lat = g.shape[2]
    part = kv.shape[0]
    n_off = len(SLOTS)
    group = math.gcd(group, heads)
    width = math.gcd(width, toks)
    steps, chunks = heads // group, toks // width
    cols, keys = group * toks, n_off * n_head * part
    rows = graw_rows(heads)
    dma = pltpu.SemaphoreType.DMA
    hbm = pl.BlockSpec(memory_space=pl.ANY)
    vmem = pl.BlockSpec(memory_space=pltpu.VMEM)
    grads = pl.pallas_call(
        functools.partial(fused_kernel, n_ctx, n_head),
        in_specs=[pl.BlockSpec(memory_space=pltpu.SMEM), hbm, hbm, hbm, hbm, hbm],
        out_specs=[vmem, vmem],
        out_shape=[
            pltpu.VMEM((steps, group, feat, toks), BF16),
            pltpu.VMEM((part, feat), BF16),
        ],
        scratch_shapes=[
            pltpu.VMEM((steps, group, feat, toks), BF16),
            pltpu.VMEM((chunks, width, heads, lat), BF16),
            pltpu.VMEM((rows, rows), BF16),
            pltpu.VMEM((steps, group, toks, lat), BF16),
            pltpu.VMEM((steps, group, toks), F32),
            pltpu.VMEM((steps, group, toks), F32),
            pltpu.VMEM((steps, keys, cols), BF16),
            pltpu.VMEM((steps, keys, cols), BF16),
            pltpu.VMEM((keys, feat), F32),
            pltpu.VMEM((n_off, n_head, part, feat), BF16),
            pltpu.VMEM((n_head - 1, n_off, part, feat), BF16),
            pltpu.VMEM((n_head - 1, n_off, part, feat), BF16),
            pltpu.VMEM((n_off - 1, part, feat), BF16),
            pltpu.VMEM((n_off - 1, part, feat), BF16),
            pltpu.VMEM((n_off - 1, n_head - 1, part, feat), BF16),
            dma((steps,)),
            dma((chunks,)),
            dma((3,)),
            dma((n_off - 1,)),
            dma((n_off - 1,)),
            dma((n_off, n_head - 1)),
            dma((n_off, n_head - 1)),
            dma((n_off, n_head - 1)),
            dma((n_off, n_head - 1)),
            dma((n_off - 1,)),
            dma((n_off - 1,)),
            dma((n_off - 1, n_head - 1)),
            dma((n_off - 1, n_head - 1)),
        ],
        compiler_params=pltpu.CompilerParams(
            collective_id=0, has_side_effects=True, vmem_limit_bytes=67043328 - 2 * heads * feat * toks - 4 * part * (feat + 128) - (1 << 18)
        ),
        cost_estimate=pl.CostEstimate(flops=12 * 10**9, bytes_accessed=14 * 10**6, transcendentals=2 * 10**6),
        name="mla_bwd",
    )(links, kv, q, g, ln.reshape(steps, group, toks), od.reshape(steps, group, toks))
    return pl.pallas_call(
        flush_kernel,
        in_specs=[vmem, vmem],
        out_specs=[hbm, hbm],
        out_shape=[
            jax.ShapeDtypeStruct((steps, group, feat, toks), BF16),
            jax.ShapeDtypeStruct((part, feat), BF16),
        ],
        scratch_shapes=[dma((steps * FLUSH + 1,))],
        compiler_params=pltpu.CompilerParams(has_side_effects=True, vmem_limit_bytes=1 << 17),
        cost_estimate=pl.CostEstimate(flops=0, bytes_accessed=10**7, transcendentals=0),
        name="flush",
    )(*[pltpu.with_memory_space_constraint(x, pltpu.VMEM) for x in grads])


def shards(q, g, ln, od, kv, links):
    dq, dkv = fused(
        lax.axis_size("ctx"),
        lax.axis_size("head"),
        jnp.transpose(q, (1, 2, 0)),
        g,
        ln.T,
        od.T,
        kv,
        links,
    )
    return jnp.transpose(dq.reshape(-1, *dq.shape[2:]), (2, 0, 1)), dkv


def solution(mesh):
    in_specs = (
        P("ctx", "head", None),
        P("ctx", "head", None),
        P("ctx", "head"),
        P("ctx", "head"),
        P(("ctx", "head"), None),
        P("ctx", None),
    )
    out_specs = (P("ctx", "head", None), P(("ctx", "head"), None))
    return jax.shard_map(shards, mesh=mesh, in_specs=in_specs, out_specs=out_specs, check_vma=False)
```

```python
import functools
import math

import jax
import jax.numpy as jnp
from jax import lax
from jax.experimental import pallas as pl
from jax.experimental.pallas import tpu as pltpu
from jax.sharding import PartitionSpec as P

F32 = jnp.float32
BF16 = jnp.bfloat16


def dot(a, b, ca, cb):
    return lax.dot_general(a, b, (((ca,), (cb,)), ((), ())), preferred_element_type=F32)


MESH = pl.DeviceIdType.MESH
TILE = 16
GROUP = 8
FLUSH = 1
PAIRED = ((2, 4), 'dq', (0, 1), (1, 2))
SLOTS = ((0, 0), (1, 1), (2, 2), (8, 3))
GO = (2, 3)
PLAN = (
    ("have", 0), ("sckt", 0, 1, 0, 2), ("relay", 2), ("hop", 0), ("relay", 3), ("sckt", 0, 1, 2, 4),
    ("have", 2), ("hop", 1), ("have", 3), ("sckt", 2, 4, 0, 4), ("fold", 3), ("fold", 2), ("have", 1),
    ("sckt", 1, 2, 0, 3), ("pass", 3), ("pass", 2), ("sckt", 1, 2, 3, 4), ("direct", 1), ("fold", 0),
    ("dq", 0, 4),
)


def fused_kernel(
    n_ctx, n_head, links_hbm, kv_hbm, q_hbm, g_hbm, ln_hbm, od_hbm,
    dqv, dkv_ref,
    links, qv, graw, perm, gv, ln_ref, od_ref, dsv, pbv, acc, kvbuf, away, yrecv, fwd, crecv, drecv,
    q_sem, g_sem, in_sem, gs_s, gs_r, fw_s, fw_r, ry_s, ry_r, rc_s, rc_r, rd_s, rd_r,
):
    me = lax.axis_index("ctx")
    head = lax.axis_index("head")
    steps, group, feat, toks = qv.shape
    chunks, width, heads, lat = graw.shape
    cols = group * toks
    n_off, _, part, _ = kvbuf.shape
    blk = n_head * part
    scale = feat ** (-0.5)
    log2e = math.log2(math.e)

    def load_g(i):
        return pltpu.make_async_copy(g_hbm.at[pl.ds(i * width, width)], graw.at[i], g_sem.at[i])

    def load_q(i):
        return pltpu.make_async_copy(q_hbm.at[pl.ds(i * group, group)], qv.at[i], q_sem.at[i])

    def loop(start, stop, body):
        def run(i, carry):
            body(i)
            return carry

        if stop > start:
            lax.fori_loop(start, stop, run, 0)

    def pairs(start, stop, body):
        whole = start + (stop - start) // 2 * 2

        def run(i, carry):
            body(start + 2 * i)
            body(start + 2 * i + 1)
            return carry

        if whole > start:
            lax.fori_loop(0, (whole - start) // 2, run, 0)
        loop(whole, stop, body)

    def peer(by, j=0):
        return (lax.rem(me + by + n_ctx, n_ctx), lax.rem(head + j + n_head, n_head))

    def send(src, dst, s_sem, r_sem, where):
        return pltpu.make_async_remote_copy(
            src_ref=src, dst_ref=dst, send_sem=s_sem, recv_sem=r_sem, device_id=where, device_id_type=MESH
        )

    own = pltpu.make_async_copy(kv_hbm, kvbuf.at[0, 0], in_sem.at[0])
    live = pltpu.make_async_copy(links_hbm, links, in_sem.at[3])
    norms = pltpu.make_async_copy(ln_hbm, ln_ref, in_sem.at[1])
    dots = pltpu.make_async_copy(od_hbm, od_ref, in_sem.at[2])

    odd = lax.rem(me, 2)
    places = [(-o, 0) for o, _ in SLOTS[2:]] + [(0, j) for j in range(1, n_head)] + [(1 - 2 * odd, 0)]
    barrier = pltpu.get_barrier_semaphore()
    for by, j in places:
        pl.semaphore_signal(barrier, inc=1, device_id=peer(by, j), device_id_type=MESH)
    for i in range(chunks):
        load_g(i).start()
    for copy in (own, live, norms, dots):
        copy.start()
    for i in range(steps):
        load_q(i).start()

    rows = perm.shape[0]
    out_row = lax.broadcasted_iota(jnp.int32, (rows, rows), 0)
    in_row = lax.broadcasted_iota(jnp.int32, (rows, rows), 1)
    in_head = lax.rem(in_row, heads)
    perm[...] = jnp.where(out_row * heads == in_head * (rows - 1) + in_row, 1.0, 0.0).astype(BF16)
    acc[...] = jnp.zeros_like(acc)

    gather = [
        send(kv_hbm, kvbuf.at[pos, 0], gs_s.at[pos - 1], gs_r.at[pos - 1], peer(SLOTS[pos][0]))
        for pos in range(1, n_off)
    ]
    spread = [
        [
            send(kv_hbm if pos == 0 else kvbuf.at[pos, 0], kvbuf.at[pos, j],
                 fw_s.at[pos, j - 1], fw_r.at[pos, j - 1], peer(0, -j))
            for j in range(1, n_head)
        ]
        for pos in range(n_off)
    ]
    pl.semaphore_wait(barrier, len(places))
    for copy in [gather[p - 1] for p in GO] + spread[0]:
        copy.start()
    hops = [
        send(kvbuf.at[2 * odd, j], kvbuf.at[1, j], gs_s.at[0] if j == 0 else fw_s.at[1, j - 1],
             gs_r.at[0] if j == 0 else fw_r.at[1, j - 1], peer(1 - 2 * odd))
        for j in range(n_head)
    ]

    def relayout(i):
        load_g(i).wait()
        size = rows // heads
        tile = max(TILE, size)
        for start in range(0, width, tile):
            parts = []
            for s in range(start, start + tile, size):
                block = graw[i, s : s + size].reshape(rows, lat)
                parts.append(dot(perm[...], block, 1, 0).reshape(heads, size, lat))
            moved = jnp.concatenate(parts, 1).astype(BF16)
            for h in range(heads):
                gv[h // group, h % group, pl.ds(pl.multiple_of(i * width + start, tile), tile), :] = moved[h]

    def scores(i, low, high):
        keys = kvbuf[low:high].reshape((high - low) * blk, feat)
        q = jnp.concatenate([qv[i, k] for k in range(group)], 1)
        g = gv[i].reshape(cols, lat)
        ln = jnp.concatenate([ln_ref[i, k : k + 1, :] for k in range(group)], 1) * log2e
        od = jnp.concatenate([od_ref[i, k : k + 1, :] for k in range(group)], 1)
        s = dot(keys, q, 1, 0)
        dp = dot(keys[:, :lat], g, 1, 1)
        ps, dss = [], []
        for pos in range(low, high):
            sl = slice((pos - low) * blk, (pos - low + 1) * blk)
            bias = jnp.where(links[0, SLOTS[pos][1]] > 0, ln, 1e30)
            p = jnp.exp2(s[sl] * (scale * log2e) - bias)
            if SLOTS[pos][0] == 0:
                key = lax.broadcasted_iota(jnp.int32, p.shape, 0) + head * part
                key = jnp.where(key >= blk, key - blk, key)
                tok = lax.rem(lax.broadcasted_iota(jnp.int32, p.shape, 1), toks)
                p = jnp.where(tok >= key, p, 0.0)
            ps.append(p.astype(BF16))
            dss.append((p * (dp[sl] - od) * scale).astype(BF16))
        return jnp.concatenate(ps, 0), jnp.concatenate(dss, 0), q, g

    def key_terms(pb, ds, q, g, low, high):
        span = slice(low * blk, high * blk)
        dk = dot(ds, q, 1, 1)
        dv = dot(pb, g, 1, 0)
        acc[span, :lat] += dk[:, :lat] + dv
        acc[span, lat:] += dk[:, lat:]

    def rows_of(pos, j):
        return acc[pos * blk + j * part : pos * blk + (j + 1) * part, :]

    across = [
        [
            send(away.at[j - 1, pos], yrecv.at[j - 1, pos], ry_s.at[pos, j - 1], ry_r.at[pos, j - 1], peer(0, j))
            for j in range(1, n_head)
        ]
        for pos in range(n_off)
    ]
    back = [
        send(fwd.at[pos - 1], crecv.at[pos - 1], rc_s.at[pos - 1], rc_r.at[pos - 1], peer(-SLOTS[pos][0]))
        for pos in range(1, n_off)
    ]
    skew = [
        [
            send(away.at[j - 1, pos], drecv.at[pos - 1, j - 1], rd_s.at[pos - 1, j - 1], rd_r.at[pos - 1, j - 1],
                 peer(-SLOTS[pos][0], j))
            for j in range(1, n_head)
        ]
        for pos in range(1, n_off)
    ]

    def start(copies):
        for copy in copies:
            copy.start()

    def arrive(copies):
        for copy in copies:
            copy.wait_recv()

    def relay(pos):
        arrive([gather[pos - 1]])
        start(spread[pos])

    def have(pos):
        arrive(hops if pos == 1 else spread[pos])

    def hop(part):
        if part == 0:
            start(hops[:1])
        else:
            start(hops[1:])

    def issue(pos):
        start([gather[pos - 1]])

    def fold(pos):
        for j in range(1, n_head):
            away[j - 1, pos] = rows_of(pos, j).astype(BF16)
        start(across[pos])

    def folded(pos):
        arrive(across[pos])
        total = rows_of(pos, 0)
        for j in range(1, n_head):
            total = total + yrecv[j - 1, pos].astype(F32)
        return total

    def onward(pos):
        fwd[pos - 1] = folded(pos).astype(BF16)
        start([back[pos - 1]])

    def direct(pos):
        for j in range(1, n_head):
            away[j - 1, pos] = rows_of(pos, j).astype(BF16)
        fwd[pos - 1] = rows_of(pos, 0).astype(BF16)
        start(skew[pos - 1] + [back[pos - 1]])

    def query(i):
        return jnp.concatenate([qv[i, k] for k in range(group)], 1)

    def sc(i, low, high):
        pb, ds, _, _ = scores(i, low, high)
        dsv[i, low * blk : high * blk, :] = ds
        pbv[i, low * blk : high * blk, :] = pb

    def sckt(i, low, high):
        pb, ds, q, g = scores(i, low, high)
        dsv[i, low * blk : high * blk, :] = ds
        key_terms(pb, ds, q, g, low, high)

    def kt(i, low, high):
        span = slice(low * blk, high * blk)
        key_terms(pbv[i, span, :], dsv[i, span, :], query(i), gv[i].reshape(cols, lat), low, high)

    def dq(i):
        keys = kvbuf[...].reshape(n_off * blk, feat)
        out = dot(keys, dsv[i], 0, 0).astype(BF16)
        for k in range(group):
            dqv[i, k] = out[:, k * toks : (k + 1) * toks]

    def scaled(part):
        return part * steps // 4

    loop(0, chunks, relayout)
    for copy in (own, live, norms, dots):
        copy.wait()
    for i in range(steps):
        load_q(i).wait()
    calls = {"relay": relay, "have": have, "fold": fold, "pass": onward, "direct": direct, "hop": hop, "issue": issue}
    loops = {"sc": sc, "kt": kt, "sckt": sckt}
    sent, got = gather[1:] + spread[0] + sum(spread[2:], []) + hops, []
    for name, *args in PLAN:
        if name == "dq":
            (pairs if 'dq' in PAIRED else loop)(scaled(args[0]), scaled(args[1]), dq)
        elif name in loops:
            low, high, first, last = args
            (pairs if (low, high) in PAIRED else loop)(scaled(first), scaled(last), lambda i, name=name, low=low, high=high: loops[name](i, low, high))
        else:
            calls[name](*args)
            pos = args[0]
            if name == "fold":
                sent += across[pos]
            elif name == "pass":
                sent, got = sent + [back[pos - 1]], got + [back[pos - 1]]
            elif name == "direct":
                both = skew[pos - 1] + [back[pos - 1]]
                sent, got = sent + both, got + both
    total = folded(0)
    for copy in sent:
        copy.wait_send()
    arrive(got)
    directs = [args[0] for name, *args in PLAN if name == "direct"]
    for pos in directs:
        for j in range(1, n_head):
            total = total + drecv[pos - 1, j - 1].astype(F32)
    for pos in range(1, n_off):
        total = total + crecv[pos - 1].astype(F32)
    dkv_ref[...] = total.astype(BF16)


def graw_rows(heads):
    return max(8, 256 // heads) * heads


def flush_kernel(dq_ref, dkv_ref, dq_hbm, dkv_hbm, sem):
    steps, group = dq_ref.shape[:2]
    size = group // FLUSH
    copies = [pltpu.make_async_copy(dkv_ref, dkv_hbm, sem.at[steps * FLUSH])]
    for i in range(steps * FLUSH):
        cut = (i // FLUSH, pl.ds(i % FLUSH * size, size))
        copies.append(pltpu.make_async_copy(dq_ref.at[cut], dq_hbm.at[cut], sem.at[i]))
    for copy in copies:
        copy.start()
    for copy in copies:
        copy.wait()


def fused(n_ctx, n_head, q, g, ln, od, kv, links, group=GROUP, width=32):
    heads, feat, toks = q.shape
    lat = g.shape[2]
    part = kv.shape[0]
    n_off = len(SLOTS)
    group = math.gcd(group, heads)
    width = math.gcd(width, toks)
    steps, chunks = heads // group, toks // width
    cols, keys = group * toks, n_off * n_head * part
    rows = graw_rows(heads)
    dma = pltpu.SemaphoreType.DMA
    hbm = pl.BlockSpec(memory_space=pl.ANY)
    vmem = pl.BlockSpec(memory_space=pltpu.VMEM)
    grads = pl.pallas_call(
        functools.partial(fused_kernel, n_ctx, n_head),
        in_specs=[hbm] * 6,
        out_specs=[vmem, vmem],
        out_shape=[
            pltpu.VMEM((steps, group, feat, toks), BF16),
            pltpu.VMEM((part, feat), BF16),
        ],
        scratch_shapes=[
            pltpu.SMEM(links.shape, jnp.int32),
            pltpu.VMEM((steps, group, feat, toks), BF16),
            pltpu.VMEM((chunks, width, heads, lat), BF16),
            pltpu.VMEM((rows, rows), BF16),
            pltpu.VMEM((steps, group, toks, lat), BF16),
            pltpu.VMEM((steps, group, toks), F32),
            pltpu.VMEM((steps, group, toks), F32),
            pltpu.VMEM((steps, keys, cols), BF16),
            pltpu.VMEM((steps, keys, cols), BF16),
            pltpu.VMEM((keys, feat), F32),
            pltpu.VMEM((n_off, n_head, part, feat), BF16),
            pltpu.VMEM((n_head - 1, n_off, part, feat), BF16),
            pltpu.VMEM((n_head - 1, n_off, part, feat), BF16),
            pltpu.VMEM((n_off - 1, part, feat), BF16),
            pltpu.VMEM((n_off - 1, part, feat), BF16),
            pltpu.VMEM((n_off - 1, n_head - 1, part, feat), BF16),
            dma((steps,)),
            dma((chunks,)),
            dma((4,)),
            dma((n_off - 1,)),
            dma((n_off - 1,)),
            dma((n_off, n_head - 1)),
            dma((n_off, n_head - 1)),
            dma((n_off, n_head - 1)),
            dma((n_off, n_head - 1)),
            dma((n_off - 1,)),
            dma((n_off - 1,)),
            dma((n_off - 1, n_head - 1)),
            dma((n_off - 1, n_head - 1)),
        ],
        compiler_params=pltpu.CompilerParams(
            collective_id=0, has_side_effects=True, vmem_limit_bytes=67043328 - 2 * heads * feat * toks - 4 * part * (feat + 128) - (1 << 18)
        ),
        cost_estimate=pl.CostEstimate(flops=12 * 10**9, bytes_accessed=14 * 10**6, transcendentals=2 * 10**6),
        name="mla_bwd",
    )(links, kv, q, g, ln.reshape(steps, group, toks), od.reshape(steps, group, toks))
    return pl.pallas_call(
        flush_kernel,
        in_specs=[vmem, vmem],
        out_specs=[hbm, hbm],
        out_shape=[
            jax.ShapeDtypeStruct((steps, group, feat, toks), BF16),
            jax.ShapeDtypeStruct((part, feat), BF16),
        ],
        scratch_shapes=[dma((steps * FLUSH + 1,))],
        compiler_params=pltpu.CompilerParams(has_side_effects=True, vmem_limit_bytes=1 << 17),
        cost_estimate=pl.CostEstimate(flops=0, bytes_accessed=10**7, transcendentals=0),
        name="flush",
    )(*[pltpu.with_memory_space_constraint(x, pltpu.VMEM) for x in grads])


def shards(q, g, ln, od, kv, links):
    dq, dkv = fused(
        lax.axis_size("ctx"),
        lax.axis_size("head"),
        jnp.transpose(q, (1, 2, 0)),
        g,
        ln.T,
        od.T,
        kv,
        links,
    )
    return jnp.transpose(dq.reshape(-1, *dq.shape[2:]), (2, 0, 1)), dkv


def solution(mesh):
    in_specs = (
        P("ctx", "head", None),
        P("ctx", "head", None),
        P("ctx", "head"),
        P("ctx", "head"),
        P(("ctx", "head"), None),
        P("ctx", None),
    )
    out_specs = (P("ctx", "head", None), P(("ctx", "head"), None))
    return jax.shard_map(shards, mesh=mesh, in_specs=in_specs, out_specs=out_specs, check_vma=False)
```

```python
import functools
import math

import jax
import jax.numpy as jnp
from jax import lax
from jax.experimental import pallas as pl
from jax.experimental.pallas import tpu as pltpu
from jax.sharding import PartitionSpec as P

F32 = jnp.float32
BF16 = jnp.bfloat16


def dot(a, b, ca, cb):
    return lax.dot_general(a, b, (((ca,), (cb,)), ((), ())), preferred_element_type=F32)


MESH = pl.DeviceIdType.MESH
TILE = 16
GROUP = 8
FLUSH = 1
PAIRED = ((2, 4), 'dq', (0, 1), (1, 2))
SLOTS = ((0, 0), (1, 1), (2, 2), (8, 3))
GO = (2, 3)
PLAN = (
    ("have", 0), ("sckt", 0, 1, 0, 2), ("relay", 2), ("hop", 0), ("relay", 3), ("sckt", 0, 1, 2, 4),
    ("have", 2), ("hop", 1), ("have", 3), ("sckt", 2, 4, 0, 4), ("direct", 2), ("fold", 3), ("have", 1),
    ("sckt", 1, 2, 0, 4), ("pass", 3), ("direct", 1), ("fold", 0), ("dq", 0, 4),
)


def fused_kernel(
    n_ctx, n_head, links_hbm, kv_hbm, q_hbm, g_hbm, ln_hbm, od_hbm,
    dqv, dkv_ref,
    links, qv, graw, perm, gv, ln_ref, od_ref, dsv, pbv, acc, kvbuf, away, yrecv, fwd, crecv, drecv,
    q_sem, g_sem, in_sem, gs_s, gs_r, fw_s, fw_r, ry_s, ry_r, rc_s, rc_r, rd_s, rd_r,
):
    me = lax.axis_index("ctx")
    head = lax.axis_index("head")
    steps, group, feat, toks = qv.shape
    chunks, width, heads, lat = graw.shape
    cols = group * toks
    n_off, _, part, _ = kvbuf.shape
    blk = n_head * part
    scale = feat ** (-0.5)
    log2e = math.log2(math.e)

    def load_g(i):
        return pltpu.make_async_copy(g_hbm.at[pl.ds(i * width, width)], graw.at[i], g_sem.at[i])

    def load_q(i):
        return pltpu.make_async_copy(q_hbm.at[pl.ds(i * group, group)], qv.at[i], q_sem.at[i])

    def loop(start, stop, body):
        def run(i, carry):
            body(i)
            return carry

        if stop > start:
            lax.fori_loop(start, stop, run, 0)

    def pairs(start, stop, body):
        whole = start + (stop - start) // 2 * 2

        def run(i, carry):
            body(start + 2 * i)
            body(start + 2 * i + 1)
            return carry

        if whole > start:
            lax.fori_loop(0, (whole - start) // 2, run, 0)
        loop(whole, stop, body)

    def peer(by, j=0):
        return (lax.rem(me + by + n_ctx, n_ctx), lax.rem(head + j + n_head, n_head))

    def send(src, dst, s_sem, r_sem, where):
        return pltpu.make_async_remote_copy(
            src_ref=src, dst_ref=dst, send_sem=s_sem, recv_sem=r_sem, device_id=where, device_id_type=MESH
        )

    own = pltpu.make_async_copy(kv_hbm, kvbuf.at[0, 0], in_sem.at[0])
    live = pltpu.make_async_copy(links_hbm, links, in_sem.at[3])
    norms = pltpu.make_async_copy(ln_hbm, ln_ref, in_sem.at[1])
    dots = pltpu.make_async_copy(od_hbm, od_ref, in_sem.at[2])

    odd = lax.rem(me, 2)
    places = [(-o, 0) for o, _ in SLOTS[2:]] + [(0, j) for j in range(1, n_head)] + [(1 - 2 * odd, 0)]
    barrier = pltpu.get_barrier_semaphore()
    for by, j in places:
        pl.semaphore_signal(barrier, inc=1, device_id=peer(by, j), device_id_type=MESH)
    for i in range(chunks):
        load_g(i).start()
    for copy in (own, live, norms, dots):
        copy.start()
    for i in range(steps):
        load_q(i).start()

    rows = perm.shape[0]
    out_row = lax.broadcasted_iota(jnp.int32, (rows, rows), 0)
    in_row = lax.broadcasted_iota(jnp.int32, (rows, rows), 1)
    in_head = lax.rem(in_row, heads)
    perm[...] = jnp.where(out_row * heads == in_head * (rows - 1) + in_row, 1.0, 0.0).astype(BF16)
    acc[...] = jnp.zeros_like(acc)

    gather = [
        send(kv_hbm, kvbuf.at[pos, 0], gs_s.at[pos - 1], gs_r.at[pos - 1], peer(SLOTS[pos][0]))
        for pos in range(1, n_off)
    ]
    spread = [
        [
            send(kv_hbm if pos == 0 else kvbuf.at[pos, 0], kvbuf.at[pos, j],
                 fw_s.at[pos, j - 1], fw_r.at[pos, j - 1], peer(0, -j))
            for j in range(1, n_head)
        ]
        for pos in range(n_off)
    ]
    pl.semaphore_wait(barrier, len(places))
    for copy in [gather[p - 1] for p in GO] + spread[0]:
        copy.start()
    hops = [
        send(kvbuf.at[2 * odd, j], kvbuf.at[1, j], gs_s.at[0] if j == 0 else fw_s.at[1, j - 1],
             gs_r.at[0] if j == 0 else fw_r.at[1, j - 1], peer(1 - 2 * odd))
        for j in range(n_head)
    ]

    def relayout(i):
        load_g(i).wait()
        size = rows // heads
        tile = max(TILE, size)
        for start in range(0, width, tile):
            parts = []
            for s in range(start, start + tile, size):
                block = graw[i, s : s + size].reshape(rows, lat)
                parts.append(dot(perm[...], block, 1, 0).reshape(heads, size, lat))
            moved = jnp.concatenate(parts, 1).astype(BF16)
            for h in range(heads):
                gv[h // group, h % group, pl.ds(pl.multiple_of(i * width + start, tile), tile), :] = moved[h]

    def scores(i, low, high):
        keys = kvbuf[low:high].reshape((high - low) * blk, feat)
        q = jnp.concatenate([qv[i, k] for k in range(group)], 1)
        g = gv[i].reshape(cols, lat)
        ln = jnp.concatenate([ln_ref[i, k : k + 1, :] for k in range(group)], 1) * log2e
        od = jnp.concatenate([od_ref[i, k : k + 1, :] for k in range(group)], 1)
        s = dot(keys, q, 1, 0)
        dp = dot(keys[:, :lat], g, 1, 1)
        ps, dss = [], []
        for pos in range(low, high):
            sl = slice((pos - low) * blk, (pos - low + 1) * blk)
            bias = jnp.where(links[0, SLOTS[pos][1]] > 0, ln, 1e30)
            p = jnp.exp2(s[sl] * (scale * log2e) - bias)
            if SLOTS[pos][0] == 0:
                key = lax.broadcasted_iota(jnp.int32, p.shape, 0) + head * part
                key = jnp.where(key >= blk, key - blk, key)
                tok = lax.rem(lax.broadcasted_iota(jnp.int32, p.shape, 1), toks)
                p = jnp.where(tok >= key, p, 0.0)
            ps.append(p.astype(BF16))
            dss.append((p * (dp[sl] - od) * scale).astype(BF16))
        return jnp.concatenate(ps, 0), jnp.concatenate(dss, 0), q, g

    def key_terms(pb, ds, q, g, low, high):
        span = slice(low * blk, high * blk)
        dk = dot(ds, q, 1, 1)
        dv = dot(pb, g, 1, 0)
        acc[span, :lat] += dk[:, :lat] + dv
        acc[span, lat:] += dk[:, lat:]

    def rows_of(pos, j):
        return acc[pos * blk + j * part : pos * blk + (j + 1) * part, :]

    across = [
        [
            send(away.at[j - 1, pos], yrecv.at[j - 1, pos], ry_s.at[pos, j - 1], ry_r.at[pos, j - 1], peer(0, j))
            for j in range(1, n_head)
        ]
        for pos in range(n_off)
    ]
    back = [
        send(fwd.at[pos - 1], crecv.at[pos - 1], rc_s.at[pos - 1], rc_r.at[pos - 1], peer(-SLOTS[pos][0]))
        for pos in range(1, n_off)
    ]
    skew = [
        [
            send(away.at[j - 1, pos], drecv.at[pos - 1, j - 1], rd_s.at[pos - 1, j - 1], rd_r.at[pos - 1, j - 1],
                 peer(-SLOTS[pos][0], j))
            for j in range(1, n_head)
        ]
        for pos in range(1, n_off)
    ]

    def start(copies):
        for copy in copies:
            copy.start()

    def arrive(copies):
        for copy in copies:
            copy.wait_recv()

    def relay(pos):
        arrive([gather[pos - 1]])
        start(spread[pos])

    def have(pos):
        arrive(hops if pos == 1 else spread[pos])

    def hop(part):
        if part == 0:
            start(hops[:1])
        else:
            start(hops[1:])

    def issue(pos):
        start([gather[pos - 1]])

    def fold(pos):
        for j in range(1, n_head):
            away[j - 1, pos] = rows_of(pos, j).astype(BF16)
        start(across[pos])

    def folded(pos):
        arrive(across[pos])
        total = rows_of(pos, 0)
        for j in range(1, n_head):
            total = total + yrecv[j - 1, pos].astype(F32)
        return total

    def onward(pos):
        fwd[pos - 1] = folded(pos).astype(BF16)
        start([back[pos - 1]])

    def direct(pos):
        for j in range(1, n_head):
            away[j - 1, pos] = rows_of(pos, j).astype(BF16)
        fwd[pos - 1] = rows_of(pos, 0).astype(BF16)
        start(skew[pos - 1] + [back[pos - 1]])

    def query(i):
        return jnp.concatenate([qv[i, k] for k in range(group)], 1)

    def sc(i, low, high):
        pb, ds, _, _ = scores(i, low, high)
        dsv[i, low * blk : high * blk, :] = ds
        pbv[i, low * blk : high * blk, :] = pb

    def sckt(i, low, high):
        pb, ds, q, g = scores(i, low, high)
        dsv[i, low * blk : high * blk, :] = ds
        key_terms(pb, ds, q, g, low, high)

    def kt(i, low, high):
        span = slice(low * blk, high * blk)
        key_terms(pbv[i, span, :], dsv[i, span, :], query(i), gv[i].reshape(cols, lat), low, high)

    def dq(i):
        keys = kvbuf[...].reshape(n_off * blk, feat)
        out = dot(keys, dsv[i], 0, 0).astype(BF16)
        for k in range(group):
            dqv[i, k] = out[:, k * toks : (k + 1) * toks]

    def scaled(part):
        return part * steps // 4

    loop(0, chunks, relayout)
    for copy in (own, live, norms, dots):
        copy.wait()
    for i in range(steps):
        load_q(i).wait()
    calls = {"relay": relay, "have": have, "fold": fold, "pass": onward, "direct": direct, "hop": hop, "issue": issue}
    loops = {"sc": sc, "kt": kt, "sckt": sckt}
    sent, got = gather[1:] + spread[0] + sum(spread[2:], []) + hops, []
    for name, *args in PLAN:
        if name == "dq":
            (pairs if 'dq' in PAIRED else loop)(scaled(args[0]), scaled(args[1]), dq)
        elif name in loops:
            low, high, first, last = args
            (pairs if (low, high) in PAIRED else loop)(scaled(first), scaled(last), lambda i, name=name, low=low, high=high: loops[name](i, low, high))
        else:
            calls[name](*args)
            pos = args[0]
            if name == "fold":
                sent += across[pos]
            elif name == "pass":
                sent, got = sent + [back[pos - 1]], got + [back[pos - 1]]
            elif name == "direct":
                both = skew[pos - 1] + [back[pos - 1]]
                sent, got = sent + both, got + both
    total = folded(0)
    for copy in sent:
        copy.wait_send()
    arrive(got)
    directs = [args[0] for name, *args in PLAN if name == "direct"]
    for pos in directs:
        for j in range(1, n_head):
            total = total + drecv[pos - 1, j - 1].astype(F32)
    for pos in range(1, n_off):
        total = total + crecv[pos - 1].astype(F32)
    dkv_ref[...] = total.astype(BF16)


def graw_rows(heads):
    return max(8, 256 // heads) * heads


def flush_kernel(dq_ref, dkv_ref, dq_hbm, dkv_hbm, sem):
    steps, group = dq_ref.shape[:2]
    size = group // FLUSH
    copies = [pltpu.make_async_copy(dkv_ref, dkv_hbm, sem.at[steps * FLUSH])]
    for i in range(steps * FLUSH):
        cut = (i // FLUSH, pl.ds(i % FLUSH * size, size))
        copies.append(pltpu.make_async_copy(dq_ref.at[cut], dq_hbm.at[cut], sem.at[i]))
    for copy in copies:
        copy.start()
    for copy in copies:
        copy.wait()


def fused(n_ctx, n_head, q, g, ln, od, kv, links, group=GROUP, width=32):
    heads, feat, toks = q.shape
    lat = g.shape[2]
    part = kv.shape[0]
    n_off = len(SLOTS)
    group = math.gcd(group, heads)
    width = math.gcd(width, toks)
    steps, chunks = heads // group, toks // width
    cols, keys = group * toks, n_off * n_head * part
    rows = graw_rows(heads)
    dma = pltpu.SemaphoreType.DMA
    hbm = pl.BlockSpec(memory_space=pl.ANY)
    vmem = pl.BlockSpec(memory_space=pltpu.VMEM)
    grads = pl.pallas_call(
        functools.partial(fused_kernel, n_ctx, n_head),
        in_specs=[hbm] * 6,
        out_specs=[vmem, vmem],
        out_shape=[
            pltpu.VMEM((steps, group, feat, toks), BF16),
            pltpu.VMEM((part, feat), BF16),
        ],
        scratch_shapes=[
            pltpu.SMEM(links.shape, jnp.int32),
            pltpu.VMEM((steps, group, feat, toks), BF16),
            pltpu.VMEM((chunks, width, heads, lat), BF16),
            pltpu.VMEM((rows, rows), BF16),
            pltpu.VMEM((steps, group, toks, lat), BF16),
            pltpu.VMEM((steps, group, toks), F32),
            pltpu.VMEM((steps, group, toks), F32),
            pltpu.VMEM((steps, keys, cols), BF16),
            pltpu.VMEM((steps, keys, cols), BF16),
            pltpu.VMEM((keys, feat), F32),
            pltpu.VMEM((n_off, n_head, part, feat), BF16),
            pltpu.VMEM((n_head - 1, n_off, part, feat), BF16),
            pltpu.VMEM((n_head - 1, n_off, part, feat), BF16),
            pltpu.VMEM((n_off - 1, part, feat), BF16),
            pltpu.VMEM((n_off - 1, part, feat), BF16),
            pltpu.VMEM((n_off - 1, n_head - 1, part, feat), BF16),
            dma((steps,)),
            dma((chunks,)),
            dma((4,)),
            dma((n_off - 1,)),
            dma((n_off - 1,)),
            dma((n_off, n_head - 1)),
            dma((n_off, n_head - 1)),
            dma((n_off, n_head - 1)),
            dma((n_off, n_head - 1)),
            dma((n_off - 1,)),
            dma((n_off - 1,)),
            dma((n_off - 1, n_head - 1)),
            dma((n_off - 1, n_head - 1)),
        ],
        compiler_params=pltpu.CompilerParams(
            collective_id=0, has_side_effects=True, vmem_limit_bytes=67043328 - 2 * heads * feat * toks - 4 * part * (feat + 128) - (1 << 18)
        ),
        cost_estimate=pl.CostEstimate(flops=12 * 10**9, bytes_accessed=14 * 10**6, transcendentals=2 * 10**6),
        name="mla_bwd",
    )(links, kv, q, g, ln.reshape(steps, group, toks), od.reshape(steps, group, toks))
    return pl.pallas_call(
        flush_kernel,
        in_specs=[vmem, vmem],
        out_specs=[hbm, hbm],
        out_shape=[
            jax.ShapeDtypeStruct((steps, group, feat, toks), BF16),
            jax.ShapeDtypeStruct((part, feat), BF16),
        ],
        scratch_shapes=[dma((steps * FLUSH + 1,))],
        compiler_params=pltpu.CompilerParams(has_side_effects=True, vmem_limit_bytes=1 << 17),
        cost_estimate=pl.CostEstimate(flops=0, bytes_accessed=10**7, transcendentals=0),
        name="flush",
    )(*[pltpu.with_memory_space_constraint(x, pltpu.VMEM) for x in grads])


def shards(q, g, ln, od, kv, links):
    dq, dkv = fused(
        lax.axis_size("ctx"),
        lax.axis_size("head"),
        jnp.transpose(q, (1, 2, 0)),
        g,
        ln.T,
        od.T,
        kv,
        links,
    )
    return jnp.transpose(dq.reshape(-1, *dq.shape[2:]), (2, 0, 1)), dkv


def solution(mesh):
    in_specs = (
        P("ctx", "head", None),
        P("ctx", "head", None),
        P("ctx", "head"),
        P("ctx", "head"),
        P(("ctx", "head"), None),
        P("ctx", None),
    )
    out_specs = (P("ctx", "head", None), P(("ctx", "head"), None))
    return jax.shard_map(shards, mesh=mesh, in_specs=in_specs, out_specs=out_specs, check_vma=False)
```
